32 devices in a mesh: slab: 32 (over z, y, x, core).
Axes of the slice: x: 2, y: 2, z: 4, core: 2. Of those that a mesh axis runs over, the one named last changes fastest.
Arguments:
- krylov_basis_block: float32 [16, 256, 16, 128], P(None, 'slab'), may hold values from -6 to 6
- companion: float32 [16, 256, 16, 128], P(None, 'slab'), may hold values from -6 to 6
- region: int32 [256, 16, 128], P('slab'), may hold values from 0 to 7
- inv_density: float32 [8], replicated, may hold values from 0.3 to 3
- stiffness: float32 [8], replicated, may hold values from 0.5 to 3
- damping: float32 [8], replicated, may hold values from 0.5 to 4
Outputs:
- new_block: float32 [16, 256, 16, 128], P(None, 'slab')
- projection: float32 [16, 16], replicated
- rfactor: float32 [16, 16], replicated
The draws below stay inside these ranges and needn't reach their ends.
All inputs are finite; a program needn't handle non-finite values.
Results may differ from the reference program's by a relative error of at most 0.00012.
Values sent between devices are 32-bit elements; how exact they have to be, the bound alone decides.
A program may use at most 64 MiB of HBM per device.

```python
import math
import jax
import jax.numpy as jnp
from jax import lax

KRYLOV_COUNT = 16
REGIONS = 8
NY = 16
NZ = 128
NX = 256


def place_ends(result, own_key, least, largest):
    longest = result.shape.index(max(result.shape))
    spots = []
    for shift in (0, 1):
        where = [jax.random.randint(jax.random.fold_in(own_key, axis), (), 0, length) for axis, length in enumerate(result.shape)]
        where[longest] = (where[longest] + shift) % result.shape[longest]
        spots.append(tuple(where))
    return result.at[spots[0]].set(least).at[spots[1]].set(largest)


def block_levels(rng, shape, shards, least, high):
    factor_of = 1.0
    for dim, shards_of in shards:
        heights = jax.random.uniform(jax.random.fold_in(jax.random.fold_in(rng, 6), dim), (shards_of,), jnp.float32, least / len(shards), high / len(shards))
        factor_of = factor_of * jnp.repeat(jnp.exp(heights), shape[dim] // shards_of).reshape((-1,) + (1,) * (len(shape) - 1 - dim))
    return factor_of


def normal_values(own_key, extent, width, reach, cuts=(), held_as=jnp.bfloat16):
    gain = block_levels(own_key, extent, cuts, -0.22, 0.18) if cuts else 1.0
    array = jax.random.normal(own_key, extent, jnp.float32) * width * gain
    return jnp.minimum(jnp.maximum(array, -reach), reach).astype(held_as)


def setup_inputs(seed: int = 0) -> dict:
    key_of = jax.random.split(jax.random.key(seed), 7)
    return {
        "krylov_basis_block": normal_values(key_of[0], (KRYLOV_COUNT, NX, NY, NZ), 1.0, 6.0, ((1, 32),), jnp.float32),
        "companion": normal_values(key_of[1], (KRYLOV_COUNT, NX, NY, NZ), 1.0, 6.0, ((1, 32),), jnp.float32),
        "region": place_ends(jax.random.randint(key_of[2], (NX, NY, NZ), 0, REGIONS), jax.random.fold_in(key_of[2], 1), 0, REGIONS - 1).astype(jnp.int32),
        "inv_density": jnp.clip(jnp.exp(jax.random.uniform(key_of[3], (REGIONS,), jnp.float32, math.log(0.3), math.log(3.0))), 0.3, 3.0),
        "stiffness": jnp.clip(jax.random.uniform(key_of[4], (REGIONS,), jnp.float32, 0.5, 3.0), 0.5, 3.0),
        "damping": jnp.clip(jnp.exp(jax.random.uniform(key_of[5], (REGIONS,), jnp.float32, math.log(0.5), math.log(4.0))), 0.5, 4.0),
    }


def lookup(region, table):
    picks = region[None] == jnp.arange(table.shape[0], dtype=jnp.int32)[:, None, None, None]
    return jnp.sum(jnp.where(picks, table[:, None, None, None], jnp.float32(0.0)), axis=0)

def operate(operator_applied, cx, mass, damp, companion):
    padded_basis = jnp.pad(operator_applied, ((0, 0), (0, 0), (1, 1), (1, 1)))
    cpad = jnp.pad(cx, ((0, 0), (1, 1), (1, 1)), mode='edge')
    center_coefficient = padded_basis[:, 1:-1, 1:-1, 1:-1]
    ccenter = cpad[1:-1, 1:-1, 1:-1]
    total = -mass * center_coefficient + damp * companion
    shifts = [(slice(2, None), slice(1, -1), slice(1, -1)), (slice(0, -2), slice(1, -1), slice(1, -1)), (slice(1, -1), slice(2, None), slice(1, -1)), (slice(1, -1), slice(0, -2), slice(1, -1)), (slice(1, -1), slice(1, -1), slice(2, None)), (slice(1, -1), slice(1, -1), slice(0, -2))]
    for selection_mask in shifts:
        neighbour_coefficient = padded_basis[:, selection_mask[0], selection_mask[1], selection_mask[2]]
        bond = 0.5 * (ccenter + cpad[selection_mask])
        total = total + bond * (center_coefficient - neighbour_coefficient)
    return total

def reference(krylov_basis_block, companion, region, inv_density, stiffness, damping):
    coef = lookup(region, inv_density)
    mass = lookup(region, stiffness)
    damp = lookup(region, damping)
    operator_applied = jnp.pad(krylov_basis_block, ((0, 0), (1, 1), (0, 0), (0, 0)))
    cx = jnp.pad(coef, ((1, 1), (0, 0), (0, 0)), mode='edge')
    fresh = operate(operator_applied, cx, mass, damp, companion)
    cell_count = NX * NY * NZ
    basis_matrix = krylov_basis_block.reshape(KRYLOV_COUNT, -1)
    image_matrix = fresh.reshape(KRYLOV_COUNT, -1)
    projection = jnp.dot(basis_matrix, image_matrix.T, precision=lax.Precision.HIGHEST) / cell_count
    reduced_products = image_matrix - jnp.dot(projection.T, basis_matrix, precision=lax.Precision.HIGHEST)
    gram = jnp.dot(reduced_products, reduced_products.T, precision=lax.Precision.HIGHEST) / cell_count
    lower = jnp.linalg.cholesky(gram)
    new_block = lax.linalg.triangular_solve(lower, reduced_products, left_side=True, lower=True)
    return (new_block.reshape(krylov_basis_block.shape), projection, lower.T)
```

```python
import functools

import jax
import jax.numpy as jnp
from jax import lax
from jax.experimental import pallas as pl
from jax.experimental.pallas import tpu as pltpu
from jax.sharding import PartitionSpec as P

AXIS = "slab"
MESH = pl.DeviceIdType.MESH
F32, BF16 = jnp.float32, jnp.bfloat16


def radices(count):
    out = []
    while count > 1:
        for r in (8, 4, 2):
            if count % r == 0:
                break
        else:
            r = next(q for q in range(3, count + 1) if count % q == 0)
        out.append(r)
        count //= r
    return out


def split3(a):
    p = a.astype(BF16)
    rest = a - p.astype(F32)
    q = rest.astype(BF16)
    return p, q, (rest - q.astype(F32)).astype(BF16)


def step_kernel(
    n, planes, ny, cells,
    b_hbm, c_hbm, reg_hbm, dens, stiff, dampt,
    out_hbm, proj_ref, rfac_ref,
    bv, cv, reg, coef, co, s, acc, ov, *rest,
):
    rads = radices(n)
    slots = rest[: len(rads)]
    load_sem, halo_send, halo_recv, reg_send, reg_recv, out_sem = rest[len(rads): len(rads) + 6]
    ph_send = rest[len(rads) + 6: 2 * len(rads) + 6]
    ph_recv = rest[2 * len(rads) + 6:]
    k = b_hbm.shape[0]
    rows = planes * ny
    span = rows + 2 * ny
    nz = b_hbm.shape[-1]
    tables = dens.shape[0]
    me = lax.axis_index(AXIS)
    has_left, has_right = me > 0, me < n - 1
    left, right = lax.rem(me + n - 1, n), lax.rem(me + 1, n)

    digits, stride = [], 1
    for r in rads:
        digits.append((stride, lax.rem(me // stride, r)))
        stride *= r

    def peer(ph, o):
        st, d = digits[ph]
        pd = lax.rem(d + o, rads[ph])
        return me + (pd - d) * st, pd

    barrier = pltpu.get_barrier_semaphore()

    @pl.when(has_left)
    def _():
        pl.semaphore_signal(barrier, inc=1, device_id=(left,), device_id_type=MESH)

    @pl.when(has_right)
    def _():
        pl.semaphore_signal(barrier, inc=1, device_id=(right,), device_id_type=MESH)

    for ph, r in enumerate(rads):
        for o in range(1, r):
            pl.semaphore_signal(barrier, inc=1, device_id=(peer(ph, o)[0],), device_id_type=MESH)

    bv3 = bv.reshape(k, span, nz)
    cp_r = pltpu.make_async_copy(reg_hbm, reg.at[pl.ds(1, planes)], load_sem.at[0])
    cp_b = pltpu.make_async_copy(b_hbm, bv3.at[:, pl.ds(ny, rows), :], load_sem.at[1])
    cp_c = pltpu.make_async_copy(c_hbm, cv.reshape(k, rows, nz), load_sem.at[2])
    cp_r.start()
    cp_b.start()
    cp_c.start()

    pl.semaphore_wait(
        barrier, sum(r - 1 for r in rads) + has_left.astype(jnp.int32) + has_right.astype(jnp.int32)
    )

    def halo(up):
        i = 0 if up else 1
        src = pl.ds(rows - ny, ny) if up else pl.ds(0, ny)
        dst = pl.ds(0, ny) if up else pl.ds(rows + ny, ny)
        to = right if up else left
        rc = pltpu.make_async_remote_copy(
            src_ref=reg_hbm.at[planes - 1 if up else 0], dst_ref=reg.at[0 if up else planes + 1],
            send_sem=reg_send.at[i], recv_sem=reg_recv.at[i],
            device_id=(to,), device_id_type=MESH)
        vc = pltpu.make_async_remote_copy(
            src_ref=b_hbm.at[:, src, :], dst_ref=bv3.at[:, dst, :],
            send_sem=halo_send.at[i], recv_sem=halo_recv.at[i],
            device_id=(to,), device_id_type=MESH)
        return rc, vc

    @pl.when(has_right)
    def _():
        for c in halo(True):
            c.start()

    @pl.when(has_left)
    def _():
        for c in halo(False):
            c.start()

    def lookup(r, table):
        out = jnp.zeros(r.shape, F32)
        for t in range(tables):
            out = jnp.where(r == t, table[t], out)
        return out

    cp_r.wait()
    coef[pl.ds(1, planes)] = lookup(reg[pl.ds(1, planes)], dens)
    cp_b.wait()
    cp_c.wait()

    lane = lax.broadcasted_iota(jnp.int32, (ny, nz), 1)
    acc[...] = jnp.zeros(acc.shape, F32)

    def plane(x):
        c = coef[x + 1]
        r = reg[x + 1]
        cxm, cxp = coef[x], coef[x + 2]
        cym = jnp.concatenate([c[:1], c[:-1]], axis=0)
        cyp = jnp.concatenate([c[1:], c[-1:]], axis=0)
        czm = jnp.where(lane == 0, c, pltpu.roll(c, 1, 1))
        czp = jnp.where(lane == nz - 1, c, pltpu.roll(c, nz - 1, 1))
        bonds = [0.5 * (c + d) for d in (cxm, cxp, cym, cyp, czm, czp)]
        co[0] = bonds[0] + bonds[1] + bonds[2] + bonds[3] + bonds[4] + bonds[5] - lookup(r, stiff)
        co[1] = lookup(r, dampt)
        for i in range(4):
            co[2 + i] = bonds[i]
        co[6] = jnp.where(lane == 0, 0.0, bonds[4])
        co[7] = jnp.where(lane == nz - 1, 0.0, bonds[5])
        base = (x + 1) * ny

        def at(row):
            return bv[pl.ds(row, k, stride=span), :]

        for y in range(ny):
            w = [jnp.broadcast_to(co[i, pl.ds(y, 1), :], (k, nz)) for i in range(8)]
            v = at(base + y)
            f = w[0] * v + w[1] * cv[pl.ds(x * ny + y, k, stride=rows), :]
            f = f - w[2] * at(base + y - ny) - w[3] * at(base + y + ny)
            if y > 0:
                f = f - w[4] * at(base + y - 1)
            if y < ny - 1:
                f = f - w[5] * at(base + y + 1)
            f = f - w[6] * pltpu.roll(v, 1, 1) - w[7] * pltpu.roll(v, nz - 1, 1)
            for i, (pb, pf) in enumerate(zip(split3(v), split3(f))):
                s[x, pl.ds(2 * k * i, k), pl.ds(y * nz, nz)] = pb
                s[x, pl.ds(2 * k * i + k, k), pl.ds(y * nz, nz)] = pf
        sx = s[x]
        acc[...] += lax.dot_general(sx, sx, (((1,), (1,)), ((), ())), preferred_element_type=F32)

    lax.fori_loop(1, planes - 1, lambda x, _: (plane(x), 0)[1], 0)

    @pl.when(has_left)
    def _():
        for c in halo(True):
            c.wait_recv()
        coef[0] = lookup(reg[0], dens)

    @pl.when(me == 0)
    def _():
        bv3[:, pl.ds(0, ny), :] = jnp.zeros((k, ny, nz), F32)
        coef[0] = coef[1]

    @pl.when(has_right)
    def _():
        for c in halo(False):
            c.wait_recv()
        coef[planes + 1] = lookup(reg[planes + 1], dens)

    @pl.when(me == n - 1)
    def _():
        bv3[:, pl.ds(rows + ny, ny), :] = jnp.zeros((k, ny, nz), F32)
        coef[planes + 1] = coef[planes]

    lax.fori_loop(0, 2, lambda i, _: (plane(i * (planes - 1)), 0)[1], 0)

    g = acc[...]
    g = g[: 2 * k] + g[2 * k: 4 * k] + g[4 * k:]
    g = g[:, : 2 * k] + g[:, 2 * k: 4 * k] + g[:, 4 * k:]
    parts = nz // (2 * k)
    tall = (2 * k) // parts
    packed = jnp.concatenate([g[i * tall: (i + 1) * tall] for i in range(parts)], axis=1)

    for ph, r in enumerate(rads):
        d = digits[ph][1]
        buf = slots[ph]
        buf[d] = packed

        def exchange(to, mine):
            return pltpu.make_async_remote_copy(
                src_ref=buf.at[d], dst_ref=buf.at[mine],
                send_sem=ph_send[ph].at[mine], recv_sem=ph_recv[ph].at[mine],
                device_id=(to,), device_id_type=MESH)

        sent = []
        for o in range(1, r):
            to, pd = peer(ph, o)
            c = pltpu.make_async_remote_copy(
                src_ref=buf.at[d], dst_ref=buf.at[d],
                send_sem=ph_send[ph].at[pd], recv_sem=ph_recv[ph].at[d],
                device_id=(to,), device_id_type=MESH)
            c.start()
            sent.append(c)
        for o in range(1, r):
            to, pd = peer(ph, o)
            exchange(to, pd).wait_recv()
        packed = buf[0]
        for i in range(1, r):
            packed = packed + buf[i]
        for c in sent:
            c.wait_send()

    packed = packed / F32(cells)
    g = jnp.concatenate([packed[:, 2 * k * i: 2 * k * (i + 1)] for i in range(parts)], axis=0)
    bb, p, pt, ff = g[:k, :k], g[:k, k:], g[k:, :k], g[k:, k:]
    dot = functools.partial(jnp.dot, precision=lax.Precision.HIGHEST, preferred_element_type=F32)
    gram = ff - dot(pt, 2.0 * p - dot(bb, p))
    proj_ref[...] = p

    ri = lax.broadcasted_iota(jnp.int32, (k, k), 0)
    ci = lax.broadcasted_iota(jnp.int32, (k, k), 1)
    m = jnp.concatenate([gram, -pt, (ri == ci).astype(F32)], axis=1)
    rid = lax.broadcasted_iota(jnp.int32, (k, 1), 0)
    for i in range(k):
        rs = lax.rsqrt(m[i: i + 1, i: i + 1])
        u = m[i: i + 1, :] * rs
        mult = jnp.where(rid > i, m[:, i: i + 1] * rs, 0.0)
        m = jnp.where(rid == i, u, m - mult * u)
    rfac_ref[...] = jnp.where(ri <= ci, m[:, :k], 0.0)

    w = jnp.concatenate(split3(m[:, k:]), axis=0)
    w = jnp.concatenate([w, w, w], axis=1)

    ov3 = ov.reshape(k, rows, nz)

    def apply(x, _):
        o = jnp.dot(w, s[x], preferred_element_type=F32)
        o = o[:k] + (o[k: 2 * k] + o[2 * k:])
        for y in range(ny):
            ov[pl.ds(x * ny + y, k, stride=rows), :] = o[:, y * nz: (y + 1) * nz]
        part = pl.ds(x * ny, ny)
        pltpu.make_async_copy(ov3.at[:, part, :], out_hbm.at[:, part, :], out_sem.at[x]).start()
        return 0

    lax.fori_loop(0, planes, apply, 0)

    @pl.when(has_right)
    def _():
        for c in halo(True):
            c.wait_send()

    @pl.when(has_left)
    def _():
        for c in halo(False):
            c.wait_send()

    for x in range(planes):
        part = pl.ds(x * ny, ny)
        pltpu.make_async_copy(ov3.at[:, part, :], out_hbm.at[:, part, :], out_sem.at[x]).wait()


def solution(mesh):
    n = mesh.shape[AXIS]
    rads = radices(n)

    def shards(b, c, region, dens, stiff, dampt):
        k, planes, ny, nz = b.shape
        rows = planes * ny
        tall = 2 * k * 2 * k // nz
        hbm = pl.BlockSpec(memory_space=pl.ANY)
        vm = pl.BlockSpec(memory_space=pltpu.VMEM)
        sm = pl.BlockSpec(memory_space=pltpu.SMEM)
        new, proj, rfac = pl.pallas_call(
            functools.partial(step_kernel, n, planes, ny, planes * ny * nz * n),
            out_shape=(
                jax.ShapeDtypeStruct((k, rows, nz), F32),
                jax.ShapeDtypeStruct((k, k), F32),
                jax.ShapeDtypeStruct((k, k), F32),
            ),
            in_specs=[hbm, hbm, hbm, sm, sm, sm],
            out_specs=(hbm, vm, vm),
            scratch_shapes=[
                pltpu.VMEM((k * (rows + 2 * ny), nz), F32),
                pltpu.VMEM((k * rows, nz), F32),
                pltpu.VMEM((planes + 2, ny, nz), jnp.int32),
                pltpu.VMEM((planes + 2, ny, nz), F32),
                pltpu.VMEM((8, ny, nz), F32),
                pltpu.VMEM((planes, 6 * k, ny * nz), BF16),
                pltpu.VMEM((6 * k, 6 * k), F32),
                pltpu.VMEM((k * rows, nz), F32),
            ]
            + [pltpu.VMEM((r, tall, nz), F32) for r in rads]
            + [
                pltpu.SemaphoreType.DMA((3,)),
                pltpu.SemaphoreType.DMA((2,)),
                pltpu.SemaphoreType.DMA((2,)),
                pltpu.SemaphoreType.DMA((2,)),
                pltpu.SemaphoreType.DMA((2,)),
                pltpu.SemaphoreType.DMA((planes,)),
            ]
            + [pltpu.SemaphoreType.DMA((r,)) for r in rads]
            + [pltpu.SemaphoreType.DMA((r,)) for r in rads],
            compiler_params=pltpu.CompilerParams(collective_id=0, has_side_effects=True),
        )(b.reshape(k, rows, nz), c.reshape(k, rows, nz), region, dens, stiff, dampt)
        return new.reshape(b.shape), proj, rfac

    placed = (
        P(None, AXIS, None, None),
        P(None, AXIS, None, None),
        P(AXIS, None, None),
        P(),
        P(),
        P(),
    )
    return jax.shard_map(
        shards,
        mesh=mesh,
        in_specs=placed,
        out_specs=(P(None, AXIS, None, None), P(), P()),
        check_vma=False,
    )
```

```python
import functools

import jax
import jax.numpy as jnp
from jax import lax
from jax.experimental import pallas as pl
from jax.experimental.pallas import tpu as pltpu
from jax.sharding import PartitionSpec as P

AXIS = "slab"
MESH = pl.DeviceIdType.MESH
F32, BF16 = jnp.float32, jnp.bfloat16


def radices(count):
    out = []
    while count > 1:
        for r in (8, 4, 2):
            if count % r == 0:
                break
        else:
            r = next(q for q in range(3, count + 1) if count % q == 0)
        out.append(r)
        count //= r
    return out


def split3(a):
    p = a.astype(BF16)
    rest = a - p.astype(F32)
    q = rest.astype(BF16)
    return p, q, (rest - q.astype(F32)).astype(BF16)


def step_kernel(
    n, planes, ny, cells,
    b_hbm, c_hbm, reg_hbm, dens, stiff, dampt,
    s, w_ref, proj_ref, rfac_ref,
    bv, cv, reg, coef, co, acc, *rest,
):
    rads = radices(n)
    slots = rest[: len(rads)]
    load_sem, halo_send, halo_recv, reg_send, reg_recv = rest[len(rads): len(rads) + 5]
    ph_send = rest[len(rads) + 5: 2 * len(rads) + 5]
    ph_recv = rest[2 * len(rads) + 5:]
    k = b_hbm.shape[0]
    rows = planes * ny
    span = rows + 2 * ny
    nz = b_hbm.shape[-1]
    tables = dens.shape[0]
    me = lax.axis_index(AXIS)
    has_left, has_right = me > 0, me < n - 1
    left, right = lax.rem(me + n - 1, n), lax.rem(me + 1, n)

    digits, stride = [], 1
    for r in rads:
        digits.append((stride, lax.rem(me // stride, r)))
        stride *= r

    def peer(ph, o):
        st, d = digits[ph]
        pd = lax.rem(d + o, rads[ph])
        return me + (pd - d) * st, pd

    barrier = pltpu.get_barrier_semaphore()

    @pl.when(has_left)
    def _():
        pl.semaphore_signal(barrier, inc=1, device_id=(left,), device_id_type=MESH)

    @pl.when(has_right)
    def _():
        pl.semaphore_signal(barrier, inc=1, device_id=(right,), device_id_type=MESH)

    for ph, r in enumerate(rads):
        for o in range(1, r):
            pl.semaphore_signal(barrier, inc=1, device_id=(peer(ph, o)[0],), device_id_type=MESH)

    bv3 = bv.reshape(k, span, nz)
    cp_r = pltpu.make_async_copy(reg_hbm, reg.at[pl.ds(1, planes)], load_sem.at[0])
    cp_b = pltpu.make_async_copy(b_hbm, bv3.at[:, pl.ds(ny, rows), :], load_sem.at[1])
    cp_c = pltpu.make_async_copy(c_hbm, cv.reshape(k, rows, nz), load_sem.at[2])
    cp_r.start()
    cp_b.start()
    cp_c.start()

    pl.semaphore_wait(
        barrier, sum(r - 1 for r in rads) + has_left.astype(jnp.int32) + has_right.astype(jnp.int32)
    )

    def halo(up):
        i = 0 if up else 1
        src = pl.ds(rows - ny, ny) if up else pl.ds(0, ny)
        dst = pl.ds(0, ny) if up else pl.ds(rows + ny, ny)
        to = right if up else left
        rc = pltpu.make_async_remote_copy(
            src_ref=reg_hbm.at[planes - 1 if up else 0], dst_ref=reg.at[0 if up else planes + 1],
            send_sem=reg_send.at[i], recv_sem=reg_recv.at[i],
            device_id=(to,), device_id_type=MESH)
        vc = pltpu.make_async_remote_copy(
            src_ref=b_hbm.at[:, src, :], dst_ref=bv3.at[:, dst, :],
            send_sem=halo_send.at[i], recv_sem=halo_recv.at[i],
            device_id=(to,), device_id_type=MESH)
        return rc, vc

    @pl.when(has_right)
    def _():
        for c in halo(True):
            c.start()

    @pl.when(has_left)
    def _():
        for c in halo(False):
            c.start()

    def lookup(r, table):
        out = jnp.zeros(r.shape, F32)
        for t in range(tables):
            out = jnp.where(r == t, table[t], out)
        return out

    cp_r.wait()
    coef[pl.ds(1, planes)] = lookup(reg[pl.ds(1, planes)], dens)
    cp_b.wait()
    cp_c.wait()

    lane = lax.broadcasted_iota(jnp.int32, (ny, nz), 1)
    acc[...] = jnp.zeros(acc.shape, F32)

    def plane(x):
        c = coef[x + 1]
        r = reg[x + 1]
        cxm, cxp = coef[x], coef[x + 2]
        cym = jnp.concatenate([c[:1], c[:-1]], axis=0)
        cyp = jnp.concatenate([c[1:], c[-1:]], axis=0)
        czm = jnp.where(lane == 0, c, pltpu.roll(c, 1, 1))
        czp = jnp.where(lane == nz - 1, c, pltpu.roll(c, nz - 1, 1))
        bonds = [0.5 * (c + d) for d in (cxm, cxp, cym, cyp, czm, czp)]
        co[0] = bonds[0] + bonds[1] + bonds[2] + bonds[3] + bonds[4] + bonds[5] - lookup(r, stiff)
        co[1] = lookup(r, dampt)
        for i in range(4):
            co[2 + i] = bonds[i]
        co[6] = jnp.where(lane == 0, 0.0, bonds[4])
        co[7] = jnp.where(lane == nz - 1, 0.0, bonds[5])
        base = (x + 1) * ny

        def at(row):
            return bv[pl.ds(row, k, stride=span), :]

        for y in range(ny):
            w = [jnp.broadcast_to(co[i, pl.ds(y, 1), :], (k, nz)) for i in range(8)]
            v = at(base + y)
            f = w[0] * v + w[1] * cv[pl.ds(x * ny + y, k, stride=rows), :]
            f = f - w[2] * at(base + y - ny) - w[3] * at(base + y + ny)
            if y > 0:
                f = f - w[4] * at(base + y - 1)
            if y < ny - 1:
                f = f - w[5] * at(base + y + 1)
            f = f - w[6] * pltpu.roll(v, 1, 1) - w[7] * pltpu.roll(v, nz - 1, 1)
            for i, (pb, pf) in enumerate(zip(split3(v), split3(f))):
                s[x, pl.ds(2 * k * i, k), pl.ds(y * nz, nz)] = pb
                s[x, pl.ds(2 * k * i + k, k), pl.ds(y * nz, nz)] = pf
        sx = s[x]
        acc[...] += lax.dot_general(sx, sx, (((1,), (1,)), ((), ())), preferred_element_type=F32)

    lax.fori_loop(1, planes - 1, lambda x, _: (plane(x), 0)[1], 0)

    @pl.when(has_left)
    def _():
        for c in halo(True):
            c.wait_recv()
        coef[0] = lookup(reg[0], dens)

    @pl.when(me == 0)
    def _():
        bv3[:, pl.ds(0, ny), :] = jnp.zeros((k, ny, nz), F32)
        coef[0] = coef[1]

    @pl.when(has_right)
    def _():
        for c in halo(False):
            c.wait_recv()
        coef[planes + 1] = lookup(reg[planes + 1], dens)

    @pl.when(me == n - 1)
    def _():
        bv3[:, pl.ds(rows + ny, ny), :] = jnp.zeros((k, ny, nz), F32)
        coef[planes + 1] = coef[planes]

    lax.fori_loop(0, 2, lambda i, _: (plane(i * (planes - 1)), 0)[1], 0)

    g = acc[...]
    g = g[: 2 * k] + g[2 * k: 4 * k] + g[4 * k:]
    g = g[:, : 2 * k] + g[:, 2 * k: 4 * k] + g[:, 4 * k:]
    parts = nz // (2 * k)
    tall = (2 * k) // parts
    packed = jnp.concatenate([g[i * tall: (i + 1) * tall] for i in range(parts)], axis=1)

    for ph, r in enumerate(rads):
        d = digits[ph][1]
        buf = slots[ph]
        buf[d] = packed

        def exchange(to, mine):
            return pltpu.make_async_remote_copy(
                src_ref=buf.at[d], dst_ref=buf.at[mine],
                send_sem=ph_send[ph].at[mine], recv_sem=ph_recv[ph].at[mine],
                device_id=(to,), device_id_type=MESH)

        sent = []
        for o in range(1, r):
            to, pd = peer(ph, o)
            c = pltpu.make_async_remote_copy(
                src_ref=buf.at[d], dst_ref=buf.at[d],
                send_sem=ph_send[ph].at[pd], recv_sem=ph_recv[ph].at[d],
                device_id=(to,), device_id_type=MESH)
            c.start()
            sent.append(c)
        for o in range(1, r):
            to, pd = peer(ph, o)
            exchange(to, pd).wait_recv()
        packed = buf[0]
        for i in range(1, r):
            packed = packed + buf[i]
        for c in sent:
            c.wait_send()

    packed = packed / F32(cells)
    g = jnp.concatenate([packed[:, 2 * k * i: 2 * k * (i + 1)] for i in range(parts)], axis=0)
    bb, p, pt, ff = g[:k, :k], g[:k, k:], g[k:, :k], g[k:, k:]
    dot = functools.partial(jnp.dot, precision=lax.Precision.HIGHEST, preferred_element_type=F32)
    gram = ff - dot(pt, 2.0 * p - dot(bb, p))
    proj_ref[...] = p

    ri = lax.broadcasted_iota(jnp.int32, (k, k), 0)
    ci = lax.broadcasted_iota(jnp.int32, (k, k), 1)
    m = jnp.concatenate([gram, -pt, (ri == ci).astype(F32)], axis=1)
    rid = lax.broadcasted_iota(jnp.int32, (k, 1), 0)
    for i in range(k):
        rs = lax.rsqrt(m[i: i + 1, i: i + 1])
        u = m[i: i + 1, :] * rs
        mult = jnp.where(rid > i, m[:, i: i + 1] * rs, 0.0)
        m = jnp.where(rid == i, u, m - mult * u)
    rfac_ref[...] = jnp.where(ri <= ci, m[:, :k], 0.0)

    w = jnp.concatenate(split3(m[:, k:]), axis=0)
    w_ref[...] = jnp.concatenate([w, w, w], axis=1)

    @pl.when(has_right)
    def _():
        for c in halo(True):
            c.wait_send()

    @pl.when(has_left)
    def _():
        for c in halo(False):
            c.wait_send()


def apply_kernel(planes, ny, s, w_ref, proj_in, rfac_in, out_hbm, proj_ref, rfac_ref, ov, out_sem):
    k = proj_in.shape[0]
    rows = planes * ny
    nz = ov.shape[-1]
    w = w_ref[...]
    ov3 = ov.reshape(k, rows, nz)

    def send(x):
        part = pl.ds(x * ny, ny)
        return pltpu.make_async_copy(ov3.at[:, part, :], out_hbm.at[:, part, :], out_sem.at[x])

    def apply(x, _):
        o = jnp.dot(w, s[x], preferred_element_type=F32)
        o = o[:k] + (o[k: 2 * k] + o[2 * k:])
        for y in range(ny):
            ov[pl.ds(x * ny + y, k, stride=rows), :] = o[:, y * nz: (y + 1) * nz]
        send(x).start()
        return 0

    lax.fori_loop(0, planes, apply, 0)
    proj_ref[...] = proj_in[...]
    rfac_ref[...] = rfac_in[...]
    for x in range(planes):
        send(x).wait()


def solution(mesh):
    n = mesh.shape[AXIS]
    rads = radices(n)

    def shards(b, c, region, dens, stiff, dampt):
        k, planes, ny, nz = b.shape
        rows = planes * ny
        tall = 2 * k * 2 * k // nz
        hbm = pl.BlockSpec(memory_space=pltpu.HBM)
        vm = pl.BlockSpec(memory_space=pltpu.VMEM)
        sm = pl.BlockSpec(memory_space=pltpu.SMEM)
        s, w, proj, rfac = pl.pallas_call(
            functools.partial(step_kernel, n, planes, ny, planes * ny * nz * n),
            out_shape=(
                pltpu.VMEM((planes, 6 * k, ny * nz), BF16),
                pltpu.VMEM((3 * k, 6 * k), BF16),
                pltpu.VMEM((k, k), F32),
                pltpu.VMEM((k, k), F32),
            ),
            in_specs=[hbm, hbm, hbm, sm, sm, sm],
            out_specs=(vm, vm, vm, vm),
            scratch_shapes=[
                pltpu.VMEM((k * (rows + 2 * ny), nz), F32),
                pltpu.VMEM((k * rows, nz), F32),
                pltpu.VMEM((planes + 2, ny, nz), jnp.int32),
                pltpu.VMEM((planes + 2, ny, nz), F32),
                pltpu.VMEM((8, ny, nz), F32),
                pltpu.VMEM((6 * k, 6 * k), F32),
            ]
            + [pltpu.VMEM((r, tall, nz), F32) for r in rads]
            + [
                pltpu.SemaphoreType.DMA((3,)),
                pltpu.SemaphoreType.DMA((2,)),
                pltpu.SemaphoreType.DMA((2,)),
                pltpu.SemaphoreType.DMA((2,)),
                pltpu.SemaphoreType.DMA((2,)),
            ]
            + [pltpu.SemaphoreType.DMA((r,)) for r in rads]
            + [pltpu.SemaphoreType.DMA((r,)) for r in rads],
            compiler_params=pltpu.CompilerParams(
                collective_id=0, has_side_effects=True, vmem_limit_bytes=60 << 20
            ),
            name="step",
        )(b.reshape(k, rows, nz), c.reshape(k, rows, nz), region, dens, stiff, dampt)
        new, proj, rfac = pl.pallas_call(
            functools.partial(apply_kernel, planes, ny),
            out_shape=(
                jax.ShapeDtypeStruct((k, rows, nz), F32),
                jax.ShapeDtypeStruct((k, k), F32),
                jax.ShapeDtypeStruct((k, k), F32),
            ),
            in_specs=[vm, vm, vm, vm],
            out_specs=(hbm, vm, vm),
            scratch_shapes=[
                pltpu.VMEM((k * rows, nz), F32),
                pltpu.SemaphoreType.DMA((planes,)),
            ],
            name="apply",
            compiler_params=pltpu.CompilerParams(vmem_limit_bytes=16 << 20),
        )(*(pltpu.with_memory_space_constraint(a, pltpu.VMEM) for a in (s, w, proj, rfac)))
        return new.reshape(b.shape), proj, rfac

    placed = (
        P(None, AXIS, None, None),
        P(None, AXIS, None, None),
        P(AXIS, None, None),
        P(),
        P(),
        P(),
    )
    return jax.shard_map(
        shards,
        mesh=mesh,
        in_specs=placed,
        out_specs=(P(None, AXIS, None, None), P(), P()),
        check_vma=False,
    )
```

```python
import functools

import jax
import jax.numpy as jnp
from jax import lax
from jax.experimental import pallas as pl
from jax.experimental.pallas import tpu as pltpu
from jax.sharding import PartitionSpec as P

AXIS = "slab"
MESH = pl.DeviceIdType.MESH
F32, BF16 = jnp.float32, jnp.bfloat16


def radices(count):
    out = []
    while count > 1:
        top = 16 if out else 2
        r = next((q for q in range(top, 1, -1) if count % q == 0), count)
        out.append(r)
        count //= r
    return out


def split3(a):
    p = a.astype(BF16)
    rest = a - p.astype(F32)
    q = rest.astype(BF16)
    return p, q, (rest - q.astype(F32)).astype(BF16)


def step_kernel(
    n, planes, ny, cells,
    b_hbm, c_hbm, reg_hbm, dens, stiff, dampt,
    s, w_ref, proj_ref, rfac_ref,
    bv, cv, reg, coef, co, acc, *rest,
):
    rads = radices(n)
    slots = rest[: len(rads)]
    load_sem, halo_send, halo_recv, reg_send, reg_recv = rest[len(rads): len(rads) + 5]
    ph_send = rest[len(rads) + 5: 2 * len(rads) + 5]
    ph_recv = rest[2 * len(rads) + 5:]
    k = b_hbm.shape[0]
    rows = planes * ny
    span = rows + 2 * ny
    nz = b_hbm.shape[-1]
    tables = dens.shape[0]
    me = lax.axis_index(AXIS)
    has_left, has_right = me > 0, me < n - 1
    left, right = lax.rem(me + n - 1, n), lax.rem(me + 1, n)

    digits, stride = [], 1
    for r in rads:
        digits.append((stride, lax.rem(me // stride, r)))
        stride *= r

    def peer(ph, o):
        st, d = digits[ph]
        pd = lax.rem(d + o, rads[ph])
        return me + (pd - d) * st, pd

    barrier = pltpu.get_barrier_semaphore()

    @pl.when(has_left)
    def _():
        pl.semaphore_signal(barrier, inc=1, device_id=(left,), device_id_type=MESH)

    @pl.when(has_right)
    def _():
        pl.semaphore_signal(barrier, inc=1, device_id=(right,), device_id_type=MESH)

    for ph, r in enumerate(rads):
        for o in range(1, r):
            pl.semaphore_signal(barrier, inc=1, device_id=(peer(ph, o)[0],), device_id_type=MESH)

    bv3 = bv.reshape(k, span, nz)
    cp_r = pltpu.make_async_copy(reg_hbm, reg.at[pl.ds(1, planes)], load_sem.at[0])
    cp_b = pltpu.make_async_copy(b_hbm, bv3.at[:, pl.ds(ny, rows), :], load_sem.at[1])
    cp_c = pltpu.make_async_copy(c_hbm, cv.reshape(k, rows, nz), load_sem.at[2])
    cp_r.start()
    cp_b.start()
    cp_c.start()

    pl.semaphore_wait(
        barrier, sum(r - 1 for r in rads) + has_left.astype(jnp.int32) + has_right.astype(jnp.int32)
    )

    def halo(up):
        i = 0 if up else 1
        src = pl.ds(rows - ny, ny) if up else pl.ds(0, ny)
        dst = pl.ds(0, ny) if up else pl.ds(rows + ny, ny)
        to = right if up else left
        rc = pltpu.make_async_remote_copy(
            src_ref=reg_hbm.at[planes - 1 if up else 0], dst_ref=reg.at[0 if up else planes + 1],
            send_sem=reg_send.at[i], recv_sem=reg_recv.at[i],
            device_id=(to,), device_id_type=MESH)
        vc = pltpu.make_async_remote_copy(
            src_ref=b_hbm.at[:, src, :], dst_ref=bv3.at[:, dst, :],
            send_sem=halo_send.at[i], recv_sem=halo_recv.at[i],
            device_id=(to,), device_id_type=MESH)
        return rc, vc

    @pl.when(has_right)
    def _():
        for c in halo(True):
            c.start()

    @pl.when(has_left)
    def _():
        for c in halo(False):
            c.start()

    def lookup(r, table):
        out = jnp.zeros(r.shape, F32)
        for t in range(tables):
            out = jnp.where(r == t, table[t], out)
        return out

    cp_r.wait()
    coef[pl.ds(1, planes)] = lookup(reg[pl.ds(1, planes)], dens)
    cp_b.wait()
    cp_c.wait()

    lane = lax.broadcasted_iota(jnp.int32, (ny, nz), 1)
    acc[...] = jnp.zeros(acc.shape, F32)

    def plane(x):
        c = coef[x + 1]
        r = reg[x + 1]
        cxm, cxp = coef[x], coef[x + 2]
        cym = jnp.concatenate([c[:1], c[:-1]], axis=0)
        cyp = jnp.concatenate([c[1:], c[-1:]], axis=0)
        czm = jnp.where(lane == 0, c, pltpu.roll(c, 1, 1))
        czp = jnp.where(lane == nz - 1, c, pltpu.roll(c, nz - 1, 1))
        bonds = [0.5 * (c + d) for d in (cxm, cxp, cym, cyp, czm, czp)]
        co[0] = bonds[0] + bonds[1] + bonds[2] + bonds[3] + bonds[4] + bonds[5] - lookup(r, stiff)
        co[1] = lookup(r, dampt)
        for i in range(4):
            co[2 + i] = bonds[i]
        co[6] = jnp.where(lane == 0, 0.0, bonds[4])
        co[7] = jnp.where(lane == nz - 1, 0.0, bonds[5])
        base = (x + 1) * ny

        def at(row):
            return bv[pl.ds(row, k, stride=span), :]

        for y in range(ny):
            w = [jnp.broadcast_to(co[i, pl.ds(y, 1), :], (k, nz)) for i in range(8)]
            v = at(base + y)
            f = w[0] * v + w[1] * cv[pl.ds(x * ny + y, k, stride=rows), :]
            f = f - w[2] * at(base + y - ny) - w[3] * at(base + y + ny)
            if y > 0:
                f = f - w[4] * at(base + y - 1)
            if y < ny - 1:
                f = f - w[5] * at(base + y + 1)
            f = f - w[6] * pltpu.roll(v, 1, 1) - w[7] * pltpu.roll(v, nz - 1, 1)
            for i, (pb, pf) in enumerate(zip(split3(v), split3(f))):
                s[x, pl.ds(2 * k * i, k), pl.ds(y * nz, nz)] = pb
                s[x, pl.ds(2 * k * i + k, k), pl.ds(y * nz, nz)] = pf
        sx = s[x]
        acc[...] += lax.dot_general(sx, sx, (((1,), (1,)), ((), ())), preferred_element_type=F32)

    lax.fori_loop(1, planes - 1, lambda x, _: (plane(x), 0)[1], 0)

    @pl.when(has_left)
    def _():
        for c in halo(True):
            c.wait_recv()
        coef[0] = lookup(reg[0], dens)

    @pl.when(me == 0)
    def _():
        bv3[:, pl.ds(0, ny), :] = jnp.zeros((k, ny, nz), F32)
        coef[0] = coef[1]

    @pl.when(has_right)
    def _():
        for c in halo(False):
            c.wait_recv()
        coef[planes + 1] = lookup(reg[planes + 1], dens)

    @pl.when(me == n - 1)
    def _():
        bv3[:, pl.ds(rows + ny, ny), :] = jnp.zeros((k, ny, nz), F32)
        coef[planes + 1] = coef[planes]

    lax.fori_loop(0, 2, lambda i, _: (plane(i * (planes - 1)), 0)[1], 0)

    g = acc[...]
    g = g[: 2 * k] + g[2 * k: 4 * k] + g[4 * k:]
    g = g[:, : 2 * k] + g[:, 2 * k: 4 * k] + g[:, 4 * k:]
    parts = nz // (2 * k)
    tall = (2 * k) // parts
    packed = jnp.concatenate([g[i * tall: (i + 1) * tall] for i in range(parts)], axis=1)

    for ph, r in enumerate(rads):
        d = digits[ph][1]
        buf = slots[ph]
        buf[d] = packed

        def exchange(to, mine):
            return pltpu.make_async_remote_copy(
                src_ref=buf.at[d], dst_ref=buf.at[mine],
                send_sem=ph_send[ph].at[mine], recv_sem=ph_recv[ph].at[mine],
                device_id=(to,), device_id_type=MESH)

        sent = []
        for o in range(1, r):
            to, pd = peer(ph, o)
            c = pltpu.make_async_remote_copy(
                src_ref=buf.at[d], dst_ref=buf.at[d],
                send_sem=ph_send[ph].at[pd], recv_sem=ph_recv[ph].at[d],
                device_id=(to,), device_id_type=MESH)
            c.start()
            sent.append(c)
        for o in range(1, r):
            to, pd = peer(ph, o)
            exchange(to, pd).wait_recv()
        packed = buf[0]
        for i in range(1, r):
            packed = packed + buf[i]
        for c in sent:
            c.wait_send()

    packed = packed / F32(cells)
    g = jnp.concatenate([packed[:, 2 * k * i: 2 * k * (i + 1)] for i in range(parts)], axis=0)
    bb, p, pt, ff = g[:k, :k], g[:k, k:], g[k:, :k], g[k:, k:]
    dot = functools.partial(jnp.dot, precision=lax.Precision.HIGHEST, preferred_element_type=F32)
    gram = ff - dot(pt, 2.0 * p - dot(bb, p))
    proj_ref[...] = p

    ri = lax.broadcasted_iota(jnp.int32, (k, k), 0)
    ci = lax.broadcasted_iota(jnp.int32, (k, k), 1)
    m = jnp.concatenate([gram, -pt, (ri == ci).astype(F32)], axis=1)
    rid = lax.broadcasted_iota(jnp.int32, (k, 1), 0)
    for i in range(k):
        rs = lax.rsqrt(m[i: i + 1, i: i + 1])
        u = m[i: i + 1, :] * rs
        mult = jnp.where(rid > i, m[:, i: i + 1] * rs, 0.0)
        m = jnp.where(rid == i, u, m - mult * u)
    rfac_ref[...] = jnp.where(ri <= ci, m[:, :k], 0.0)

    w = jnp.concatenate(split3(m[:, k:]), axis=0)
    w_ref[...] = jnp.concatenate([w, w, w], axis=1)

    @pl.when(has_right)
    def _():
        for c in halo(True):
            c.wait_send()

    @pl.when(has_left)
    def _():
        for c in halo(False):
            c.wait_send()


def apply_kernel(planes, ny, s, w_ref, proj_in, rfac_in, out_hbm, proj_ref, rfac_ref, ov, out_sem):
    k = proj_in.shape[0]
    rows = planes * ny
    nz = ov.shape[-1]
    w = w_ref[...]
    ov3 = ov.reshape(k, rows, nz)

    def send(x):
        part = pl.ds(x * ny, ny)
        return pltpu.make_async_copy(ov3.at[:, part, :], out_hbm.at[:, part, :], out_sem.at[x])

    def apply(x, _):
        o = jnp.dot(w, s[x], preferred_element_type=F32)
        o = o[:k] + (o[k: 2 * k] + o[2 * k:])
        for y in range(ny):
            ov[pl.ds(x * ny + y, k, stride=rows), :] = o[:, y * nz: (y + 1) * nz]
        send(x).start()
        return 0

    lax.fori_loop(0, planes, apply, 0, unroll=True)
    proj_ref[...] = proj_in[...]
    rfac_ref[...] = rfac_in[...]
    for x in range(planes):
        send(x).wait()


def solution(mesh):
    n = mesh.shape[AXIS]
    rads = radices(n)

    def shards(b, c, region, dens, stiff, dampt):
        k, planes, ny, nz = b.shape
        rows = planes * ny
        tall = 2 * k * 2 * k // nz
        hbm = pl.BlockSpec(memory_space=pltpu.HBM)
        vm = pl.BlockSpec(memory_space=pltpu.VMEM)
        sm = pl.BlockSpec(memory_space=pltpu.SMEM)
        s, w, proj, rfac = pl.pallas_call(
            functools.partial(step_kernel, n, planes, ny, planes * ny * nz * n),
            out_shape=(
                pltpu.VMEM((planes, 6 * k, ny * nz), BF16),
                pltpu.VMEM((3 * k, 6 * k), BF16),
                pltpu.VMEM((k, k), F32),
                pltpu.VMEM((k, k), F32),
            ),
            in_specs=[hbm, hbm, hbm, sm, sm, sm],
            out_specs=(vm, vm, vm, vm),
            scratch_shapes=[
                pltpu.VMEM((k * (rows + 2 * ny), nz), F32),
                pltpu.VMEM((k * rows, nz), F32),
                pltpu.VMEM((planes + 2, ny, nz), jnp.int32),
                pltpu.VMEM((planes + 2, ny, nz), F32),
                pltpu.VMEM((8, ny, nz), F32),
                pltpu.VMEM((6 * k, 6 * k), F32),
            ]
            + [pltpu.VMEM((r, tall, nz), F32) for r in rads]
            + [
                pltpu.SemaphoreType.DMA((3,)),
                pltpu.SemaphoreType.DMA((2,)),
                pltpu.SemaphoreType.DMA((2,)),
                pltpu.SemaphoreType.DMA((2,)),
                pltpu.SemaphoreType.DMA((2,)),
            ]
            + [pltpu.SemaphoreType.DMA((r,)) for r in rads]
            + [pltpu.SemaphoreType.DMA((r,)) for r in rads],
            compiler_params=pltpu.CompilerParams(
                collective_id=0, has_side_effects=True, vmem_limit_bytes=60 << 20
            ),
            name="step",
        )(b.reshape(k, rows, nz), c.reshape(k, rows, nz), region, dens, stiff, dampt)
        new, proj, rfac = pl.pallas_call(
            functools.partial(apply_kernel, planes, ny),
            out_shape=(
                jax.ShapeDtypeStruct((k, rows, nz), F32),
                jax.ShapeDtypeStruct((k, k), F32),
                jax.ShapeDtypeStruct((k, k), F32),
            ),
            in_specs=[vm, vm, vm, vm],
            out_specs=(hbm, vm, vm),
            scratch_shapes=[
                pltpu.VMEM((k * rows, nz), F32),
                pltpu.SemaphoreType.DMA((planes,)),
            ],
            name="apply",
            compiler_params=pltpu.CompilerParams(vmem_limit_bytes=16 << 20),
        )(*(pltpu.with_memory_space_constraint(a, pltpu.VMEM) for a in (s, w, proj, rfac)))
        return new.reshape(b.shape), proj, rfac

    placed = (
        P(None, AXIS, None, None),
        P(None, AXIS, None, None),
        P(AXIS, None, None),
        P(),
        P(),
        P(),
    )
    return jax.shard_map(
        shards,
        mesh=mesh,
        in_specs=placed,
        out_specs=(P(None, AXIS, None, None), P(), P()),
        check_vma=False,
    )
```

```python
import functools

import jax
import jax.numpy as jnp
from jax import lax
from jax.experimental import pallas as pl
from jax.experimental.pallas import tpu as pltpu
from jax.sharding import PartitionSpec as P

AXIS = "slab"
MESH = pl.DeviceIdType.MESH
F32, BF16 = jnp.float32, jnp.bfloat16


def radices(count):
    out = []
    while count > 1:
        top = 16 if out else 2
        r = next((q for q in range(top, 1, -1) if count % q == 0), count)
        out.append(r)
        count //= r
    return out


def split3(a):
    p = a.astype(BF16)
    rest = a - p.astype(F32)
    q = rest.astype(BF16)
    return p, q, (rest - q.astype(F32)).astype(BF16)


def step_kernel(
    n, planes, ny, cells,
    b_hbm, c_hbm, reg_hbm, dens, stiff, dampt,
    s, w_ref, proj_ref, rfac_ref,
    bv, cv, reg, coef, co, acc, fe, ready, *rest,
):
    rads = radices(n)
    slots = rest[: len(rads)]
    load_sem, halo_send, halo_recv, reg_send, reg_recv = rest[len(rads): len(rads) + 5]
    ph_send = rest[len(rads) + 5: 2 * len(rads) + 5]
    ph_recv = rest[2 * len(rads) + 5:]
    k = b_hbm.shape[0]
    rows = planes * ny
    span = rows + 2 * ny
    nz = b_hbm.shape[-1]
    tables = dens.shape[0]
    me = lax.axis_index(AXIS)
    has_left, has_right = me > 0, me < n - 1
    left, right = lax.rem(me + n - 1, n), lax.rem(me + 1, n)

    digits, stride = [], 1
    for r in rads:
        digits.append((stride, lax.rem(me // stride, r)))
        stride *= r

    def peer(ph, o):
        st, d = digits[ph]
        pd = lax.rem(d + o, rads[ph])
        return me + (pd - d) * st, pd

    near, far = [], []
    for r, (st, _) in zip(rads, digits):
        inner = next((q for q in (4, 2) if r > 4 and r % q == 0), r)
        near.append((st, inner))
        if inner < r:
            near.append((st * inner, r // inner))
            far.append((st * inner, r // inner))

    def members(st, r):
        d = lax.rem(me // st, r)
        return [me + (lax.rem(d + o, r) - d) * st for o in range(1, r)]

    barrier = pltpu.get_barrier_semaphore()

    @pl.when(has_left)
    def _():
        pl.semaphore_signal(barrier, inc=1, device_id=(left,), device_id_type=MESH)

    @pl.when(has_right)
    def _():
        pl.semaphore_signal(barrier, inc=1, device_id=(right,), device_id_type=MESH)

    greeted = 0
    for st, r in near:
        for to in members(st, r):
            pl.semaphore_signal(barrier, inc=1, device_id=(to,), device_id_type=MESH)
            greeted += 1

    bv3 = bv.reshape(k, span, nz)
    cp_r = pltpu.make_async_copy(reg_hbm, reg.at[pl.ds(1, planes)], load_sem.at[0])
    cp_b = pltpu.make_async_copy(b_hbm, bv3.at[:, pl.ds(ny, rows), :], load_sem.at[1])
    cp_c = pltpu.make_async_copy(c_hbm, cv.reshape(k, rows, nz), load_sem.at[2])
    cp_r.start()
    cp_b.start()
    cp_c.start()

    pl.semaphore_wait(
        barrier, greeted + has_left.astype(jnp.int32) + has_right.astype(jnp.int32)
    )

    def halo(up):
        i = 0 if up else 1
        src = pl.ds(rows - ny, ny) if up else pl.ds(0, ny)
        dst = pl.ds(0, ny) if up else pl.ds(rows + ny, ny)
        to = right if up else left
        rc = pltpu.make_async_remote_copy(
            src_ref=reg_hbm.at[planes - 1 if up else 0], dst_ref=reg.at[0 if up else planes + 1],
            send_sem=reg_send.at[i], recv_sem=reg_recv.at[i],
            device_id=(to,), device_id_type=MESH)
        vc = pltpu.make_async_remote_copy(
            src_ref=b_hbm.at[:, src, :], dst_ref=bv3.at[:, dst, :],
            send_sem=halo_send.at[i], recv_sem=halo_recv.at[i],
            device_id=(to,), device_id_type=MESH)
        return rc, vc

    @pl.when(has_right)
    def _():
        for c in halo(True):
            c.start()

    @pl.when(has_left)
    def _():
        for c in halo(False):
            c.start()

    for i, (st, r) in enumerate(far):
        for to in members(st, r):
            pl.semaphore_signal(ready.at[i], inc=1, device_id=(to,), device_id_type=MESH)

    def lookup(r, table):
        out = jnp.zeros(r.shape, F32)
        for t in range(tables):
            out = jnp.where(r == t, table[t], out)
        return out

    cp_r.wait()
    coef[pl.ds(1, planes)] = lookup(reg[pl.ds(1, planes)], dens)
    cp_b.wait()
    cp_c.wait()

    lane = lax.broadcasted_iota(jnp.int32, (ny, nz), 1)
    acc[...] = jnp.zeros(acc.shape, F32)

    def plane(x, edge=None):
        c = coef[x + 1]
        r = reg[x + 1]
        cxm = c if edge == 0 else coef[x]
        cxp = c if edge == 1 else coef[x + 2]
        cym = jnp.concatenate([c[:1], c[:-1]], axis=0)
        cyp = jnp.concatenate([c[1:], c[-1:]], axis=0)
        czm = jnp.where(lane == 0, c, pltpu.roll(c, 1, 1))
        czp = jnp.where(lane == nz - 1, c, pltpu.roll(c, nz - 1, 1))
        bonds = [0.5 * (c + d) for d in (cxm, cxp, cym, cyp, czm, czp)]
        if edge is not None:
            bonds[edge] = jnp.zeros_like(c)
        co[0] = bonds[0] + bonds[1] + bonds[2] + bonds[3] + bonds[4] + bonds[5] - lookup(r, stiff)
        co[1] = lookup(r, dampt)
        for i in range(4):
            co[2 + i] = bonds[i]
        co[6] = jnp.where(lane == 0, 0.0, bonds[4])
        co[7] = jnp.where(lane == nz - 1, 0.0, bonds[5])
        base = (x + 1) * ny

        def at(row):
            return bv[pl.ds(row, k, stride=span), :]

        for y in range(ny):
            w = [jnp.broadcast_to(co[i, pl.ds(y, 1), :], (k, nz)) for i in range(8)]
            v = at(base + y)
            f = w[0] * v + w[1] * cv[pl.ds(x * ny + y, k, stride=rows), :]
            if edge != 0:
                f = f - w[2] * at(base + y - ny)
            if edge != 1:
                f = f - w[3] * at(base + y + ny)
            if y > 0:
                f = f - w[4] * at(base + y - 1)
            if y < ny - 1:
                f = f - w[5] * at(base + y + 1)
            f = f - w[6] * pltpu.roll(v, 1, 1) - w[7] * pltpu.roll(v, nz - 1, 1)
            for i, pb in enumerate(split3(v)):
                s[x, pl.ds(2 * k * i, k), pl.ds(y * nz, nz)] = pb
            if edge is None:
                put(x, y, f)
            else:
                fe[edge, pl.ds(y * k, k), :] = f
        if edge is None:
            gram_of(x)

    def put(x, y, f):
        for i, pf in enumerate(split3(f)):
            s[x, pl.ds(2 * k * i + k, k), pl.ds(y * nz, nz)] = pf

    def finish(x, edge):
        co[edge] = 0.5 * (coef[x + 1] + coef[x + 2 * edge])
        row = (x + 1) * ny
        halo_row = (x + 2 * edge) * ny
        for y in range(ny):
            w = jnp.broadcast_to(co[edge, pl.ds(y, 1), :], (k, nz))
            v = bv[pl.ds(row + y, k, stride=span), :] - bv[pl.ds(halo_row + y, k, stride=span), :]
            put(x, y, fe[edge, pl.ds(y * k, k), :] + w * v)
        gram_of(x)

    def gram_of(x):
        sx = s[x]
        acc[...] += lax.dot_general(sx, sx, (((1,), (1,)), ((), ())), preferred_element_type=F32)

    lax.fori_loop(1, planes - 1, lambda x, _: (plane(x), 0)[1], 0, unroll=2)
    plane(0, 0)
    plane(planes - 1, 1)

    @pl.when(has_left)
    def _():
        for c in halo(True):
            c.wait_recv()
        coef[0] = lookup(reg[0], dens)

    @pl.when(me == 0)
    def _():
        bv3[:, pl.ds(0, ny), :] = jnp.zeros((k, ny, nz), F32)
        coef[0] = coef[1]

    @pl.when(has_right)
    def _():
        for c in halo(False):
            c.wait_recv()
        coef[planes + 1] = lookup(reg[planes + 1], dens)

    @pl.when(me == n - 1)
    def _():
        bv3[:, pl.ds(rows + ny, ny), :] = jnp.zeros((k, ny, nz), F32)
        coef[planes + 1] = coef[planes]

    finish(0, 0)
    finish(planes - 1, 1)

    g = acc[...]
    g = g[: 2 * k] + g[2 * k: 4 * k] + g[4 * k:]
    g = g[:, : 2 * k] + g[:, 2 * k: 4 * k] + g[:, 4 * k:]
    parts = nz // (2 * k)
    tall = (2 * k) // parts
    packed = jnp.concatenate([g[i * tall: (i + 1) * tall] for i in range(parts)], axis=1)

    for i, (st, r) in enumerate(far):
        pl.semaphore_wait(ready.at[i], r - 1)

    for ph, r in enumerate(rads):
        d = digits[ph][1]
        buf = slots[ph]
        buf[d] = packed

        def exchange(to, mine):
            return pltpu.make_async_remote_copy(
                src_ref=buf.at[d], dst_ref=buf.at[mine],
                send_sem=ph_send[ph].at[mine], recv_sem=ph_recv[ph].at[mine],
                device_id=(to,), device_id_type=MESH)

        sent = []
        for o in range(1, r):
            to, pd = peer(ph, o)
            c = pltpu.make_async_remote_copy(
                src_ref=buf.at[d], dst_ref=buf.at[d],
                send_sem=ph_send[ph].at[pd], recv_sem=ph_recv[ph].at[d],
                device_id=(to,), device_id_type=MESH)
            c.start()
            sent.append(c)
        for o in range(1, r):
            to, pd = peer(ph, o)
            exchange(to, pd).wait_recv()
        packed = buf[0]
        for i in range(1, r):
            packed = packed + buf[i]
        for c in sent:
            c.wait_send()

    packed = packed / F32(cells)
    g = jnp.concatenate([packed[:, 2 * k * i: 2 * k * (i + 1)] for i in range(parts)], axis=0)
    bb, p, pt, ff = g[:k, :k], g[:k, k:], g[k:, :k], g[k:, k:]
    dot = functools.partial(jnp.dot, precision=lax.Precision.HIGHEST, preferred_element_type=F32)
    gram = ff - dot(pt, 2.0 * p - dot(bb, p))
    proj_ref[...] = p

    ri = lax.broadcasted_iota(jnp.int32, (k, k), 0)
    ci = lax.broadcasted_iota(jnp.int32, (k, k), 1)
    m = jnp.concatenate([gram, -pt, (ri == ci).astype(F32)], axis=1)
    rid = lax.broadcasted_iota(jnp.int32, (k, 1), 0)
    for i in range(k):
        rs = lax.rsqrt(m[i: i + 1, i: i + 1])
        u = m[i: i + 1, :] * rs
        mult = jnp.where(rid > i, m[:, i: i + 1] * rs, 0.0)
        m = jnp.where(rid == i, u, m - mult * u)
    rfac_ref[...] = jnp.where(ri <= ci, m[:, :k], 0.0)

    w = jnp.concatenate(split3(m[:, k:]), axis=0)
    w_ref[...] = jnp.concatenate([w, w, w], axis=1)

    @pl.when(has_right)
    def _():
        for c in halo(True):
            c.wait_send()

    @pl.when(has_left)
    def _():
        for c in halo(False):
            c.wait_send()


def apply_kernel(planes, ny, s, w_ref, proj_in, rfac_in, out_hbm, proj_ref, rfac_ref, ov, out_sem):
    k = proj_in.shape[0]
    rows = planes * ny
    nz = ov.shape[-1]
    w = w_ref[...]
    ov3 = ov.reshape(k, rows, nz)

    def send(x):
        part = pl.ds(x * ny, ny)
        return pltpu.make_async_copy(ov3.at[:, part, :], out_hbm.at[:, part, :], out_sem.at[x])

    def apply(x, _):
        o = jnp.dot(w, s[x], preferred_element_type=F32)
        o = o[:k] + (o[k: 2 * k] + o[2 * k:])
        for y in range(ny):
            ov[pl.ds(x * ny + y, k, stride=rows), :] = o[:, y * nz: (y + 1) * nz]
        send(x).start()
        return 0

    lax.fori_loop(0, planes, apply, 0, unroll=True)
    proj_ref[...] = proj_in[...]
    rfac_ref[...] = rfac_in[...]
    for x in range(planes):
        send(x).wait()


def solution(mesh):
    n = mesh.shape[AXIS]
    rads = radices(n)

    def shards(b, c, region, dens, stiff, dampt):
        k, planes, ny, nz = b.shape
        rows = planes * ny
        tall = 2 * k * 2 * k // nz
        hbm = pl.BlockSpec(memory_space=pltpu.HBM)
        vm = pl.BlockSpec(memory_space=pltpu.VMEM)
        sm = pl.BlockSpec(memory_space=pltpu.SMEM)
        s, w, proj, rfac = pl.pallas_call(
            functools.partial(step_kernel, n, planes, ny, planes * ny * nz * n),
            out_shape=(
                pltpu.VMEM((planes, 6 * k, ny * nz), BF16),
                pltpu.VMEM((3 * k, 6 * k), BF16),
                pltpu.VMEM((k, k), F32),
                pltpu.VMEM((k, k), F32),
            ),
            in_specs=[hbm, hbm, hbm, sm, sm, sm],
            out_specs=(vm, vm, vm, vm),
            scratch_shapes=[
                pltpu.VMEM((k * (rows + 2 * ny), nz), F32),
                pltpu.VMEM((k * rows, nz), F32),
                pltpu.VMEM((planes + 2, ny, nz), jnp.int32),
                pltpu.VMEM((planes + 2, ny, nz), F32),
                pltpu.VMEM((8, ny, nz), F32),
                pltpu.VMEM((6 * k, 6 * k), F32),
                pltpu.VMEM((2, ny * k, nz), F32),
                pltpu.SemaphoreType.REGULAR((len(rads),)),
            ]
            + [pltpu.VMEM((r, tall, nz), F32) for r in rads]
            + [
                pltpu.SemaphoreType.DMA((3,)),
                pltpu.SemaphoreType.DMA((2,)),
                pltpu.SemaphoreType.DMA((2,)),
                pltpu.SemaphoreType.DMA((2,)),
                pltpu.SemaphoreType.DMA((2,)),
            ]
            + [pltpu.SemaphoreType.DMA((r,)) for r in rads]
            + [pltpu.SemaphoreType.DMA((r,)) for r in rads],
            compiler_params=pltpu.CompilerParams(
                collective_id=0, has_side_effects=True, vmem_limit_bytes=60 << 20
            ),
            name="step",
        )(b.reshape(k, rows, nz), c.reshape(k, rows, nz), region, dens, stiff, dampt)
        new, proj, rfac = pl.pallas_call(
            functools.partial(apply_kernel, planes, ny),
            out_shape=(
                jax.ShapeDtypeStruct((k, rows, nz), F32),
                jax.ShapeDtypeStruct((k, k), F32),
                jax.ShapeDtypeStruct((k, k), F32),
            ),
            in_specs=[vm, vm, vm, vm],
            out_specs=(hbm, vm, vm),
            scratch_shapes=[
                pltpu.VMEM((k * rows, nz), F32),
                pltpu.SemaphoreType.DMA((planes,)),
            ],
            name="apply",
            compiler_params=pltpu.CompilerParams(vmem_limit_bytes=16 << 20),
        )(*(pltpu.with_memory_space_constraint(a, pltpu.VMEM) for a in (s, w, proj, rfac)))
        return new.reshape(b.shape), proj, rfac

    placed = (
        P(None, AXIS, None, None),
        P(None, AXIS, None, None),
        P(AXIS, None, None),
        P(),
        P(),
        P(),
    )
    return jax.shard_map(
        shards,
        mesh=mesh,
        in_specs=placed,
        out_specs=(P(None, AXIS, None, None), P(), P()),
        check_vma=False,
    )
```

```python
import functools

import jax
import jax.numpy as jnp
from jax import lax
from jax.experimental import pallas as pl
from jax.experimental.pallas import tpu as pltpu
from jax.sharding import PartitionSpec as P

AXIS = "slab"
MESH = pl.DeviceIdType.MESH
F32, BF16 = jnp.float32, jnp.bfloat16


def radices(count):
    out = []
    while count > 1:
        top = 16 if out else 2
        r = next((q for q in range(top, 1, -1) if count % q == 0), count)
        out.append(r)
        count //= r
    return out


def split3(a):
    p = a.astype(BF16)
    rest = a - p.astype(F32)
    q = rest.astype(BF16)
    return p, q, (rest - q.astype(F32)).astype(BF16)


def step_kernel(
    n, planes, ny, cells,
    b_hbm, c_hbm, reg_hbm, dens, stiff, dampt,
    s, w_ref, proj_ref, rfac_ref,
    bv, cv, reg, coef, co, acc, fe, ready, *rest,
):
    rads = radices(n)
    slots = rest[: len(rads)]
    load_sem, halo_send, halo_recv, reg_send, reg_recv = rest[len(rads): len(rads) + 5]
    ph_send = rest[len(rads) + 5: 2 * len(rads) + 5]
    ph_recv = rest[2 * len(rads) + 5:]
    k = b_hbm.shape[0]
    rows = planes * ny
    span = rows + 2 * ny
    nz = b_hbm.shape[-1]
    tables = dens.shape[0]
    me = lax.axis_index(AXIS)
    has_left, has_right = me > 0, me < n - 1
    left, right = lax.rem(me + n - 1, n), lax.rem(me + 1, n)

    digits, stride = [], 1
    for r in rads:
        digits.append((stride, lax.rem(me // stride, r)))
        stride *= r

    def peer(ph, o):
        st, d = digits[ph]
        pd = lax.rem(d + o, rads[ph])
        return me + (pd - d) * st, pd

    near, far = [], []
    for r, (st, _) in zip(rads, digits):
        inner = next((q for q in (4, 2) if r > 4 and r % q == 0), r)
        near.append((st, inner))
        if inner < r:
            near.append((st * inner, r // inner))
            far.append((st * inner, r // inner))

    def members(st, r):
        d = lax.rem(me // st, r)
        return [me + (lax.rem(d + o, r) - d) * st for o in range(1, r)]

    barrier = pltpu.get_barrier_semaphore()

    @pl.when(has_left)
    def _():
        pl.semaphore_signal(barrier, inc=1, device_id=(left,), device_id_type=MESH)

    @pl.when(has_right)
    def _():
        pl.semaphore_signal(barrier, inc=1, device_id=(right,), device_id_type=MESH)

    greeted = 0
    for st, r in near:
        for to in members(st, r):
            pl.semaphore_signal(barrier, inc=1, device_id=(to,), device_id_type=MESH)
            greeted += 1

    bv3 = bv.reshape(k, span, nz)
    cp_r = pltpu.make_async_copy(reg_hbm, reg.at[pl.ds(1, planes)], load_sem.at[0])
    cp_b = pltpu.make_async_copy(b_hbm, bv3.at[:, pl.ds(ny, rows), :], load_sem.at[1])
    cp_c = pltpu.make_async_copy(c_hbm, cv.reshape(k, rows, nz), load_sem.at[2])
    cp_r.start()
    cp_b.start()
    cp_c.start()

    def lookup(r, table):
        out = jnp.zeros(r.shape, F32)
        for t in range(tables):
            out = jnp.where(r == t, table[t], out)
        return out

    cp_r.wait()
    coef[pl.ds(1, planes)] = lookup(reg[pl.ds(1, planes)], dens)
    pl.semaphore_wait(
        barrier, greeted + has_left.astype(jnp.int32) + has_right.astype(jnp.int32)
    )

    def halo(up):
        i = 0 if up else 1
        src = pl.ds(rows - ny, ny) if up else pl.ds(0, ny)
        dst = pl.ds(0, ny) if up else pl.ds(rows + ny, ny)
        to = right if up else left
        rc = pltpu.make_async_remote_copy(
            src_ref=reg_hbm.at[planes - 1 if up else 0], dst_ref=reg.at[0 if up else planes + 1],
            send_sem=reg_send.at[i], recv_sem=reg_recv.at[i],
            device_id=(to,), device_id_type=MESH)
        vc = pltpu.make_async_remote_copy(
            src_ref=b_hbm.at[:, src, :], dst_ref=bv3.at[:, dst, :],
            send_sem=halo_send.at[i], recv_sem=halo_recv.at[i],
            device_id=(to,), device_id_type=MESH)
        return rc, vc

    @pl.when(has_right)
    def _():
        for c in halo(True):
            c.start()

    @pl.when(has_left)
    def _():
        for c in halo(False):
            c.start()

    for i, (st, r) in enumerate(far):
        for to in members(st, r):
            pl.semaphore_signal(ready.at[i], inc=1, device_id=(to,), device_id_type=MESH)

    cp_b.wait()
    cp_c.wait()

    lane = lax.broadcasted_iota(jnp.int32, (ny, nz), 1)
    acc[...] = jnp.zeros(acc.shape, F32)

    def plane(x, edge=None):
        c = coef[x + 1]
        r = reg[x + 1]
        cxm = c if edge == 0 else coef[x]
        cxp = c if edge == 1 else coef[x + 2]
        cym = jnp.concatenate([c[:1], c[:-1]], axis=0)
        cyp = jnp.concatenate([c[1:], c[-1:]], axis=0)
        czm = jnp.where(lane == 0, c, pltpu.roll(c, 1, 1))
        czp = jnp.where(lane == nz - 1, c, pltpu.roll(c, nz - 1, 1))
        bonds = [0.5 * (c + d) for d in (cxm, cxp, cym, cyp, czm, czp)]
        if edge is not None:
            bonds[edge] = jnp.zeros_like(c)
        co[0] = bonds[0] + bonds[1] + bonds[2] + bonds[3] + bonds[4] + bonds[5] - lookup(r, stiff)
        co[1] = lookup(r, dampt)
        for i in range(4):
            co[2 + i] = bonds[i]
        co[6] = jnp.where(lane == 0, 0.0, bonds[4])
        co[7] = jnp.where(lane == nz - 1, 0.0, bonds[5])
        base = (x + 1) * ny

        def at(row):
            return bv[pl.ds(row, k, stride=span), :]

        for y in range(ny):
            w = [jnp.broadcast_to(co[i, pl.ds(y, 1), :], (k, nz)) for i in range(8)]
            v = at(base + y)
            f = w[0] * v + w[1] * cv[pl.ds(x * ny + y, k, stride=rows), :]
            if edge != 0:
                f = f - w[2] * at(base + y - ny)
            if edge != 1:
                f = f - w[3] * at(base + y + ny)
            if y > 0:
                f = f - w[4] * at(base + y - 1)
            if y < ny - 1:
                f = f - w[5] * at(base + y + 1)
            f = f - w[6] * pltpu.roll(v, 1, 1) - w[7] * pltpu.roll(v, nz - 1, 1)
            for i, pb in enumerate(split3(v)):
                s[x, pl.ds(2 * k * i, k), pl.ds(y * nz, nz)] = pb
            if edge is None:
                put(x, y, f)
            else:
                fe[edge, pl.ds(y * k, k), :] = f
        if edge is None:
            gram_of(x)

    def put(x, y, f):
        for i, pf in enumerate(split3(f)):
            s[x, pl.ds(2 * k * i + k, k), pl.ds(y * nz, nz)] = pf

    def finish(x, edge):
        co[edge] = 0.5 * (coef[x + 1] + coef[x + 2 * edge])
        row = (x + 1) * ny
        halo_row = (x + 2 * edge) * ny
        for y in range(ny):
            w = jnp.broadcast_to(co[edge, pl.ds(y, 1), :], (k, nz))
            v = bv[pl.ds(row + y, k, stride=span), :] - bv[pl.ds(halo_row + y, k, stride=span), :]
            put(x, y, fe[edge, pl.ds(y * k, k), :] + w * v)
        gram_of(x)

    def gram_of(x):
        sx = s[x]
        acc[...] += lax.dot_general(sx, sx, (((1,), (1,)), ((), ())), preferred_element_type=F32)

    lax.fori_loop(1, planes - 1, lambda x, _: (plane(x), 0)[1], 0, unroll=2)
    plane(0, 0)
    plane(planes - 1, 1)

    @pl.when(has_left)
    def _():
        for c in halo(True):
            c.wait_recv()
        coef[0] = lookup(reg[0], dens)

    @pl.when(me == 0)
    def _():
        bv3[:, pl.ds(0, ny), :] = jnp.zeros((k, ny, nz), F32)
        coef[0] = coef[1]

    @pl.when(has_right)
    def _():
        for c in halo(False):
            c.wait_recv()
        coef[planes + 1] = lookup(reg[planes + 1], dens)

    @pl.when(me == n - 1)
    def _():
        bv3[:, pl.ds(rows + ny, ny), :] = jnp.zeros((k, ny, nz), F32)
        coef[planes + 1] = coef[planes]

    finish(0, 0)
    finish(planes - 1, 1)

    g = acc[...]
    g = g[: 2 * k] + g[2 * k: 4 * k] + g[4 * k:]
    g = g[:, : 2 * k] + g[:, 2 * k: 4 * k] + g[:, 4 * k:]
    parts = nz // (2 * k)
    tall = (2 * k) // parts
    packed = jnp.concatenate([g[i * tall: (i + 1) * tall] for i in range(parts)], axis=1)

    for i, (st, r) in enumerate(far):
        pl.semaphore_wait(ready.at[i], r - 1)

    for ph, r in enumerate(rads):
        d = digits[ph][1]
        buf = slots[ph]
        buf[d] = packed

        def exchange(to, mine):
            return pltpu.make_async_remote_copy(
                src_ref=buf.at[d], dst_ref=buf.at[mine],
                send_sem=ph_send[ph].at[mine], recv_sem=ph_recv[ph].at[mine],
                device_id=(to,), device_id_type=MESH)

        sent = []
        for o in range(1, r):
            to, pd = peer(ph, o)
            c = pltpu.make_async_remote_copy(
                src_ref=buf.at[d], dst_ref=buf.at[d],
                send_sem=ph_send[ph].at[pd], recv_sem=ph_recv[ph].at[d],
                device_id=(to,), device_id_type=MESH)
            c.start()
            sent.append(c)
        for o in range(1, r):
            to, pd = peer(ph, o)
            exchange(to, pd).wait_recv()
        packed = buf[0]
        for i in range(1, r):
            packed = packed + buf[i]
        for c in sent:
            c.wait_send()

    packed = packed / F32(cells)
    g = jnp.concatenate([packed[:, 2 * k * i: 2 * k * (i + 1)] for i in range(parts)], axis=0)
    bb, p, pt, ff = g[:k, :k], g[:k, k:], g[k:, :k], g[k:, k:]
    dot = functools.partial(jnp.dot, precision=lax.Precision.HIGHEST, preferred_element_type=F32)
    gram = ff - dot(pt, 2.0 * p - dot(bb, p))
    proj_ref[...] = p

    ri = lax.broadcasted_iota(jnp.int32, (k, k), 0)
    ci = lax.broadcasted_iota(jnp.int32, (k, k), 1)
    m = jnp.concatenate([gram, -pt, (ri == ci).astype(F32)], axis=1)
    rid = lax.broadcasted_iota(jnp.int32, (k, 1), 0)
    for i in range(k):
        rs = lax.rsqrt(m[i: i + 1, i: i + 1])
        u = m[i: i + 1, :] * rs
        mult = jnp.where(rid > i, m[:, i: i + 1] * rs, 0.0)
        m = jnp.where(rid == i, u, m - mult * u)
    rfac_ref[...] = jnp.where(ri <= ci, m[:, :k], 0.0)

    w = jnp.concatenate(split3(m[:, k:]), axis=0)
    w_ref[...] = jnp.concatenate([w, w, w], axis=1)

    @pl.when(has_right)
    def _():
        for c in halo(True):
            c.wait_send()

    @pl.when(has_left)
    def _():
        for c in halo(False):
            c.wait_send()


def apply_kernel(planes, ny, s, w_ref, proj_in, rfac_in, out_hbm, proj_ref, rfac_ref, ov, out_sem):
    k = proj_in.shape[0]
    rows = planes * ny
    nz = ov.shape[-1]
    w = w_ref[...]
    ov3 = ov.reshape(k, rows, nz)

    def send(x):
        part = pl.ds(x * ny, ny)
        return pltpu.make_async_copy(ov3.at[:, part, :], out_hbm.at[:, part, :], out_sem.at[x])

    def apply(x, _):
        o = jnp.dot(w, s[x], preferred_element_type=F32)
        o = o[:k] + (o[k: 2 * k] + o[2 * k:])
        for y in range(ny):
            ov[pl.ds(x * ny + y, k, stride=rows), :] = o[:, y * nz: (y + 1) * nz]
        send(x).start()
        return 0

    lax.fori_loop(0, planes, apply, 0, unroll=True)
    proj_ref[...] = proj_in[...]
    rfac_ref[...] = rfac_in[...]
    for x in range(planes):
        send(x).wait()


def solution(mesh):
    n = mesh.shape[AXIS]
    rads = radices(n)

    def shards(b, c, region, dens, stiff, dampt):
        k, planes, ny, nz = b.shape
        rows = planes * ny
        tall = 2 * k * 2 * k // nz
        hbm = pl.BlockSpec(memory_space=pltpu.HBM)
        vm = pl.BlockSpec(memory_space=pltpu.VMEM)
        sm = pl.BlockSpec(memory_space=pltpu.SMEM)
        s, w, proj, rfac = pl.pallas_call(
            functools.partial(step_kernel, n, planes, ny, planes * ny * nz * n),
            out_shape=(
                pltpu.VMEM((planes, 6 * k, ny * nz), BF16),
                pltpu.VMEM((3 * k, 6 * k), BF16),
                pltpu.VMEM((k, k), F32),
                pltpu.VMEM((k, k), F32),
            ),
            in_specs=[hbm, hbm, hbm, sm, sm, sm],
            out_specs=(vm, vm, vm, vm),
            scratch_shapes=[
                pltpu.VMEM((k * (rows + 2 * ny), nz), F32),
                pltpu.VMEM((k * rows, nz), F32),
                pltpu.VMEM((planes + 2, ny, nz), jnp.int32),
                pltpu.VMEM((planes + 2, ny, nz), F32),
                pltpu.VMEM((8, ny, nz), F32),
                pltpu.VMEM((6 * k, 6 * k), F32),
                pltpu.VMEM((2, ny * k, nz), F32),
                pltpu.SemaphoreType.REGULAR((len(rads),)),
            ]
            + [pltpu.VMEM((r, tall, nz), F32) for r in rads]
            + [
                pltpu.SemaphoreType.DMA((3,)),
                pltpu.SemaphoreType.DMA((2,)),
                pltpu.SemaphoreType.DMA((2,)),
                pltpu.SemaphoreType.DMA((2,)),
                pltpu.SemaphoreType.DMA((2,)),
            ]
            + [pltpu.SemaphoreType.DMA((r,)) for r in rads]
            + [pltpu.SemaphoreType.DMA((r,)) for r in rads],
            compiler_params=pltpu.CompilerParams(
                collective_id=0, has_side_effects=True, vmem_limit_bytes=60 << 20
            ),
            name="step",
        )(b.reshape(k, rows, nz), c.reshape(k, rows, nz), region, dens, stiff, dampt)
        new, proj, rfac = pl.pallas_call(
            functools.partial(apply_kernel, planes, ny),
            out_shape=(
                jax.ShapeDtypeStruct((k, rows, nz), F32),
                jax.ShapeDtypeStruct((k, k), F32),
                jax.ShapeDtypeStruct((k, k), F32),
            ),
            in_specs=[vm, vm, vm, vm],
            out_specs=(hbm, vm, vm),
            scratch_shapes=[
                pltpu.VMEM((k * rows, nz), F32),
                pltpu.SemaphoreType.DMA((planes,)),
            ],
            name="apply",
            compiler_params=pltpu.CompilerParams(vmem_limit_bytes=16 << 20),
        )(*(pltpu.with_memory_space_constraint(a, pltpu.VMEM) for a in (s, w, proj, rfac)))
        return new.reshape(b.shape), proj, rfac

    placed = (
        P(None, AXIS, None, None),
        P(None, AXIS, None, None),
        P(AXIS, None, None),
        P(),
        P(),
        P(),
    )
    return jax.shard_map(
        shards,
        mesh=mesh,
        in_specs=placed,
        out_specs=(P(None, AXIS, None, None), P(), P()),
        check_vma=False,
    )
```
